32 devices in a mesh: ctx: 8 (over z, x), fsdp: 4 (over y, core).
Axes of the slice: x: 2, y: 2, z: 4, core: 2. Of those that a mesh axis runs over, the one named last changes fastest.
Arguments:
- tokens: bfloat16 [4, 1024, 640], P('fsdp', 'ctx'), as said below
- pair_table: int32 [8], replicated, may hold values from 0 to 7, each once
- cotangent: bfloat16 [4, 1024, 640], P('fsdp', 'ctx'), may hold values from -6 to 6
- heads_weight: bfloat16 [1536, 640], P(('ctx', 'fsdp')), may hold values from -0.25 to 0.25
- merge_weight: bfloat16 [1024, 640], P(('ctx', 'fsdp')), may hold values from -0.1875 to 0.1875
- gate_weight: bfloat16 [2048, 640], P(('ctx', 'fsdp')), may hold values from -0.25 to 0.25
- up_weight: bfloat16 [2048, 640], P(('ctx', 'fsdp')), may hold values from -0.25 to 0.25
- down_weight: bfloat16 [2048, 640], P(('ctx', 'fsdp')), may hold values from -0.125 to 0.125
- norm_gains: bfloat16 [3072], P(('ctx', 'fsdp')), may hold values from 0.5 to 1.5
- heads_first: float32 [1536, 640], P(('ctx', 'fsdp')), may hold values from -60 to 60
- heads_second: float32 [1536, 640], P(('ctx', 'fsdp')), may hold values from 30 to 3000
- merge_first: float32 [1024, 640], P(('ctx', 'fsdp')), may hold values from -60 to 60
- merge_second: float32 [1024, 640], P(('ctx', 'fsdp')), may hold values from 30 to 3000
- gate_first: float32 [2048, 640], P(('ctx', 'fsdp')), may hold values from -60 to 60
- gate_second: float32 [2048, 640], P(('ctx', 'fsdp')), may hold values from 30 to 3000
- up_first: float32 [2048, 640], P(('ctx', 'fsdp')), may hold values from -60 to 60
- up_second: float32 [2048, 640], P(('ctx', 'fsdp')), may hold values from 30 to 3000
- down_first: float32 [2048, 640], P(('ctx', 'fsdp')), may hold values from -60 to 60
- down_second: float32 [2048, 640], P(('ctx', 'fsdp')), may hold values from 30 to 3000
- gains_first: float32 [3072], P(('ctx', 'fsdp')), may hold values from -60 to 60
- gains_second: float32 [3072], P(('ctx', 'fsdp')), may hold values from 30 to 3000
Outputs:
- mixed: bfloat16 [4, 1024, 640], P('fsdp', 'ctx')
- tokens_gradient: float32 [4, 1024, 640], P('fsdp', 'ctx')
- heads_gradient: float32 [1536, 640], P(('ctx', 'fsdp'))
- heads_update: float32 [1536, 640], P(('ctx', 'fsdp'))
- heads_moment: float32 [1536, 640], P(('ctx', 'fsdp'))
- heads_variance: float32 [1536, 640], P(('ctx', 'fsdp'))
- merge_gradient: float32 [1024, 640], P(('ctx', 'fsdp'))
- merge_update: float32 [1024, 640], P(('ctx', 'fsdp'))
- merge_moment: float32 [1024, 640], P(('ctx', 'fsdp'))
- merge_variance: float32 [1024, 640], P(('ctx', 'fsdp'))
- gate_gradient: float32 [2048, 640], P(('ctx', 'fsdp'))
- gate_update: float32 [2048, 640], P(('ctx', 'fsdp'))
- gate_moment: float32 [2048, 640], P(('ctx', 'fsdp'))
- gate_variance: float32 [2048, 640], P(('ctx', 'fsdp'))
- up_gradient: float32 [2048, 640], P(('ctx', 'fsdp'))
- up_update: float32 [2048, 640], P(('ctx', 'fsdp'))
- up_moment: float32 [2048, 640], P(('ctx', 'fsdp'))
- up_variance: float32 [2048, 640], P(('ctx', 'fsdp'))
- down_gradient: float32 [2048, 640], P(('ctx', 'fsdp'))
- down_update: float32 [2048, 640], P(('ctx', 'fsdp'))
- down_moment: float32 [2048, 640], P(('ctx', 'fsdp'))
- down_variance: float32 [2048, 640], P(('ctx', 'fsdp'))
- gains_gradient: float32 [3072], P(('ctx', 'fsdp'))
- gains_update: float32 [3072], P(('ctx', 'fsdp'))
- gains_moment: float32 [3072], P(('ctx', 'fsdp'))
- gains_variance: float32 [3072], P(('ctx', 'fsdp'))
The draws below stay inside these ranges and needn't reach their ends.
Inputs may be any that keep to these rules, and one draw needn't show every extreme that they name: Ctx index c holds position blocks pair_table[c] and 15 - pair_table[c] of its sequence; every value appears once. `tokens`: real-valued activations.
All inputs are finite; a program needn't handle non-finite values.
Results may differ from the reference program's by a relative error of at most 0.019.
Values may be sent and summed in bfloat16 or wider, within the bound.
No kernel may reach another device: no remote copies, remote signals or barrier semaphores. Data moves between devices by JAX's collectives and lax.ppermute only.
A program may use at most 128 MiB of HBM per device.

```python
import math
import jax
import jax.numpy as jnp
from jax import lax

D = 640
HEADS = 4
HD = 256
FF = 2048
TOK_DEV = 128
STEP = 3
SEQ = 1024
SEQS = 4
GAINS = 3072
N_CTX = 8


def draw_tokens(key, part):
    key_rows = jax.random.fold_in(key, 11)
    key_cols = jax.random.fold_in(key, 12)
    key_vals = jax.random.fold_in(key, 13)
    row_scale = jnp.exp(jax.random.uniform(key_rows, (SEQS, SEQ, 1), jnp.float32, math.log(0.3), math.log(3.0)))
    col_scale = jnp.exp(jax.random.uniform(key_cols, (1, 1, D), jnp.float32, math.log(0.5), math.log(2.0)))
    base = jax.random.normal(key_vals, (SEQS, SEQ, D), jnp.float32)
    return (base * row_scale * col_scale).astype(jnp.bfloat16)


def steps_of(stream_key, shape, pieces, low, high):
    def one(position, blocks):
        steps = jax.random.uniform(jax.random.fold_in(jax.random.fold_in(stream_key, 6), position), (blocks,), jnp.float32, low / len(pieces), high / len(pieces))
        return jnp.repeat(jnp.exp(steps), shape[position] // blocks).reshape((-1,) + (1,) * (len(shape) - position - 1))

    gain = one(*pieces[0])
    for cut in pieces[1:]:
        gain = gain * one(*cut)
    return gain


def bell_draw(rng, dims, scale, limit, cuts=(), held_as=jnp.bfloat16):
    entries = jax.random.normal(rng, dims, jnp.float32) * scale
    if len(cuts) > 0:
        entries = steps_of(rng, dims, cuts, -0.22, 0.18) * entries
    return jnp.clip(entries, min=-limit, max=limit).astype(held_as)


def setup_inputs(seed: int = 0) -> dict:
    splits = jax.random.split(jax.random.key(seed), 22)
    return {
        "tokens": draw_tokens(jax.random.fold_in(splits[21], 71), 0),
        "pair_table": jax.random.permutation(splits[1], N_CTX).astype(jnp.int32),
        "cotangent": bell_draw(splits[2], (SEQS, SEQ, D), 1.0, 6.0, ((0, 4), (1, 8))),
        "heads_weight": bell_draw(splits[3], ((HEADS + 2) * HD, D), D ** -0.5, 0.25, ((0, 32),)),
        "merge_weight": bell_draw(splits[4], (HEADS * HD, D), (HEADS * HD) ** -0.5, 0.1875, ((0, 32),)),
        "gate_weight": bell_draw(splits[5], (FF, D), D ** -0.5, 0.25, ((0, 32),)),
        "up_weight": bell_draw(splits[6], (FF, D), D ** -0.5, 0.25, ((0, 32),)),
        "down_weight": bell_draw(splits[7], (FF, D), FF ** -0.5, 0.125, ((0, 32),)),
        "norm_gains": jnp.clip(1.0 + 0.1 * jax.random.normal(splits[8], (GAINS,), jnp.float32), 0.5, 1.5).astype(jnp.bfloat16),
        "heads_first": bell_draw(splits[9], ((HEADS + 2) * HD, D), 10.0, 60.0, ((0, 32),), jnp.float32),
        "heads_second": jnp.clip(jnp.exp(math.log(3000.0) - 4.6051702 * jax.random.uniform(splits[10], ((HEADS + 2) * HD, D), jnp.float32) ** steps_of(splits[10], ((HEADS + 2) * HD, D), ((0, 32),), -0.2, 0.2)), 30.0, 3000.0),
        "merge_first": bell_draw(splits[11], (HEADS * HD, D), 10.0, 60.0, ((0, 32),), jnp.float32),
        "merge_second": jnp.clip(jnp.exp(math.log(3000.0) - 4.6051702 * jax.random.uniform(splits[12], (HEADS * HD, D), jnp.float32) ** steps_of(splits[12], (HEADS * HD, D), ((0, 32),), -0.2, 0.2)), 30.0, 3000.0),
        "gate_first": bell_draw(splits[13], (FF, D), 10.0, 60.0, ((0, 32),), jnp.float32),
        "gate_second": jnp.clip(jnp.exp(math.log(3000.0) - 4.6051702 * jax.random.uniform(splits[14], (FF, D), jnp.float32) ** steps_of(splits[14], (FF, D), ((0, 32),), -0.2, 0.2)), 30.0, 3000.0),
        "up_first": bell_draw(splits[15], (FF, D), 10.0, 60.0, ((0, 32),), jnp.float32),
        "up_second": jnp.clip(jnp.exp(math.log(3000.0) - 4.6051702 * jax.random.uniform(splits[16], (FF, D), jnp.float32) ** steps_of(splits[16], (FF, D), ((0, 32),), -0.2, 0.2)), 30.0, 3000.0),
        "down_first": bell_draw(splits[17], (FF, D), 10.0, 60.0, ((0, 32),), jnp.float32),
        "down_second": jnp.clip(jnp.exp(math.log(3000.0) - 4.6051702 * jax.random.uniform(splits[18], (FF, D), jnp.float32) ** steps_of(splits[18], (FF, D), ((0, 32),), -0.2, 0.2)), 30.0, 3000.0),
        "gains_first": bell_draw(splits[19], (GAINS,), 10.0, 60.0, ((0, 32),), jnp.float32),
        "gains_second": jnp.clip(jnp.exp(math.log(3000.0) - 4.6051702 * jax.random.uniform(splits[20], (GAINS,), jnp.float32) ** steps_of(splits[20], (GAINS,), ((0, 32),), -0.2, 0.2)), 30.0, 3000.0),
    }


highest = lax.Precision.HIGHEST
norm_eps = 1e-06
rope_base = 1000000.0
score_scale = 0.0625
masked_score = -1e+30
beta_one = 0.9
beta_two = 0.95
learn_rate = 0.02
weight_decay = 0.1
adam_eps = 1e-08

@jax.custom_vjp
def low(v):
    return lax.optimization_barrier(v.astype(jnp.bfloat16)).astype(jnp.float32)

@jax.custom_vjp
def low_back(v):
    return v

def low_keep(v):
    return (low(v), None)

def low_pass(kept, grad):
    return (grad,)

def back_keep(v):
    return (v, None)

def back_low(kept, grad):
    return (low(grad),)
low.defvjp(low_keep, low_pass)
low_back.defvjp(back_keep, back_low)

def product(former, latter):
    return jnp.dot(former, latter, precision=highest, preferred_element_type=jnp.float32)

def normalize(values, norm_gain):
    return values * lax.rsqrt(lax.optimization_barrier(jnp.mean(values * values, axis=-1, keepdims=True)) + norm_eps) * norm_gain

def rotary(values, positions):
    extent = values.shape[-1]
    half_width = extent // 2
    frequency = rope_base ** (-(jnp.arange(half_width, dtype=jnp.float32) * 2.0 / extent))
    angles = positions.astype(jnp.float32)[:, None] * frequency[None, :]
    target_shape = (values.shape[0],) + (1,) * (values.ndim - 2) + (extent,)
    cosine_part = jnp.concatenate([jnp.cos(angles), jnp.cos(angles)], axis=-1).reshape(target_shape)
    sine_part = jnp.concatenate([jnp.sin(angles), jnp.sin(angles)], axis=-1).reshape(target_shape)
    turned = jnp.concatenate([-values[..., half_width:], values[..., :half_width]], axis=-1)
    return values * cosine_part + turned * sine_part

def attention(queries, key_rows, value_rows):
    seq_len = key_rows.shape[0]
    block_rows = min(512, seq_len)
    block_count = seq_len // block_rows
    key_places = jnp.arange(seq_len, dtype=jnp.int32)

    def one_block(operands):
        query_block, first_row = operands
        scores = jnp.einsum('qhd,kd->hqk', query_block, key_rows, precision=highest) * score_scale
        scores = low_back(scores)
        allowed = key_places[None, :] <= (first_row + jnp.arange(block_rows, dtype=jnp.int32))[:, None]
        scores = jnp.where(allowed[None], scores, masked_score)
        weights = low(jax.nn.softmax(scores, axis=-1))
        mixture = jnp.einsum('hqk,kd->qhd', weights, value_rows, precision=highest)
        return mixture.reshape(block_rows, HEADS * HD)
    starts = jnp.arange(block_count, dtype=jnp.int32) * block_rows
    blocks = lax.map(jax.checkpoint(one_block), (queries.reshape(block_count, block_rows, HEADS, HD), starts))
    return blocks.reshape(seq_len, HEADS * HD)

def layer(sequence, params):
    heads_matrix, merge_matrix, gate_matrix, up_matrix, down_matrix, gain_vector = params
    seq_len = sequence.shape[0]
    places = jnp.arange(seq_len, dtype=jnp.int32)
    normed = low(normalize(sequence, gain_vector[0:D]))
    projected = low_back(product(normed, heads_matrix.T))
    queries = projected[:, :HEADS * HD].reshape(seq_len, HEADS, HD)
    queries = low(rotary(normalize(queries, gain_vector[4 * D:4 * D + HD]), places))
    key_rows = low(rotary(normalize(projected[:, HEADS * HD:(HEADS + 1) * HD], gain_vector[4 * D + HD:]), places))
    value_rows = low(projected[:, (HEADS + 1) * HD:])
    attended = low_back(low(attention(queries, key_rows, value_rows)))
    branch = low_back(product(attended, merge_matrix))
    residual = sequence + normalize(branch, gain_vector[D:2 * D])
    normed_ffn = low(normalize(residual, gain_vector[2 * D:3 * D]))
    gate_values = low_back(product(normed_ffn, gate_matrix.T))
    upward = low_back(product(normed_ffn, up_matrix.T))
    hidden = low(jax.nn.gelu(gate_values, approximate=True) * upward)
    output = low_back(product(hidden, down_matrix))
    return residual + normalize(output, gain_vector[3 * D:4 * D])

def adamw(weight, gradient, momentum, variance):
    moment_new = beta_one * momentum + (1.0 - beta_one) * gradient
    variance_new = beta_two * variance + (1.0 - beta_two) * gradient * gradient
    corrected = moment_new / (1.0 - beta_one ** STEP)
    spread = jnp.sqrt(variance_new / (1.0 - beta_two ** STEP))
    update = -learn_rate * (corrected / (spread + adam_eps) + weight_decay * weight)
    return (gradient, update, moment_new, variance_new)

def reference(tokens, pair_table, cotangent, heads_weight, merge_weight, gate_weight, up_weight, down_weight, norm_gains, heads_first, heads_second, merge_first, merge_second, gate_first, gate_second, up_first, up_second, down_first, down_second, gains_first, gains_second):
    half_len = TOK_DEV // 2
    stored_block = jnp.stack([pair_table, 2 * N_CTX - 1 - pair_table], axis=1).reshape(-1).astype(jnp.int32)
    stored_place = (stored_block[:, None] * half_len + jnp.arange(half_len, dtype=jnp.int32)[None, :]).reshape(-1).astype(jnp.int32)
    to_place = jnp.argsort(stored_place).astype(jnp.int32)
    params = tuple((weight.astype(jnp.float32) for weight in (heads_weight, merge_weight, gate_weight, up_weight, down_weight, norm_gains)))
    inputs_placed = tokens.astype(jnp.float32)[:, to_place]

    def forward(all_inputs, params):

        def one_sequence(carried, sequence):
            return (carried, layer(sequence, params))
        return lax.scan(one_sequence, jnp.zeros((), jnp.float32), all_inputs)[1]
    outputs, pullback = jax.vjp(forward, inputs_placed, params)
    input_gradient, weight_gradients = pullback(cotangent.astype(jnp.float32)[:, to_place])
    mixed = outputs[:, stored_place].astype(jnp.bfloat16)
    tokens_gradient = input_gradient[:, stored_place]
    heads_out = adamw(params[0], weight_gradients[0], heads_first, heads_second)
    merge_out = adamw(params[1], weight_gradients[1], merge_first, merge_second)
    gate_out = adamw(params[2], weight_gradients[2], gate_first, gate_second)
    up_out = adamw(params[3], weight_gradients[3], up_first, up_second)
    down_out = adamw(params[4], weight_gradients[4], down_first, down_second)
    gains_out = adamw(params[5], weight_gradients[5], gains_first, gains_second)
    return (mixed, tokens_gradient, heads_out[0], heads_out[1], heads_out[2], heads_out[3], merge_out[0], merge_out[1], merge_out[2], merge_out[3], gate_out[0], gate_out[1], gate_out[2], gate_out[3], up_out[0], up_out[1], up_out[2], up_out[3], down_out[0], down_out[1], down_out[2], down_out[3], gains_out[0], gains_out[1], gains_out[2], gains_out[3])
```

```python
import jax
import jax.numpy as jnp
from jax import lax
from jax.sharding import PartitionSpec as P

D = 640
HEADS = 4
HD = 256
STEP = 3


norm_eps = 1e-06
rope_base = 1000000.0
score_scale = 0.0625
masked_score = -1e30
beta_one = 0.9
beta_two = 0.95
learn_rate = 0.02
weight_decay = 0.1
adam_eps = 1e-08


def normalize(values, norm_gain):
    return (
        values * lax.rsqrt(jnp.mean(values * values, axis=-1, keepdims=True) + norm_eps) * norm_gain
    )


def rotary(values, positions):
    extent = values.shape[-1]
    half_width = extent // 2
    frequency = rope_base ** (-(jnp.arange(half_width, dtype=jnp.float32) * 2.0 / extent))
    angles = positions.astype(jnp.float32)[:, None] * frequency[None, :]
    target_shape = (values.shape[0],) + (1,) * (values.ndim - 2) + (extent,)
    cosine_part = jnp.concatenate([jnp.cos(angles), jnp.cos(angles)], axis=-1).reshape(target_shape)
    sine_part = jnp.concatenate([jnp.sin(angles), jnp.sin(angles)], axis=-1).reshape(target_shape)
    turned = jnp.concatenate([-values[..., half_width:], values[..., :half_width]], axis=-1)
    return values * cosine_part + turned * sine_part


def matmul(former, latter):
    return jnp.dot(former, latter, preferred_element_type=jnp.float32)


def contract_rows(former, latter):
    return lax.dot_general(
        former, latter, (((0,), (0,)), ((), ())), preferred_element_type=jnp.float32
    )


def contract_cols(former, latter):
    return lax.dot_general(
        former, latter, (((1,), (1,)), ((), ())), preferred_element_type=jnp.float32
    )


def adamw(weight, gradient, momentum, variance):
    moment_new = beta_one * momentum + (1.0 - beta_one) * gradient
    variance_new = beta_two * variance + (1.0 - beta_two) * gradient * gradient
    corrected = moment_new / (1.0 - beta_one**STEP)
    spread = jnp.sqrt(variance_new / (1.0 - beta_two**STEP))
    update = -learn_rate * (
        corrected / (spread + adam_eps) + weight_decay * weight.astype(jnp.float32)
    )
    return (gradient, update, moment_new, variance_new)


longest_ring = 4


def exchange(values, axis, step):
    return lax.ppermute(values, axis, [(i, i ^ step) for i in range(lax.axis_size(axis))])


def shift(values, axis, step):
    size = lax.axis_size(axis)
    return lax.ppermute(values, axis, [(i, (i + step) % size) for i in range(size)])


def piece_holders():
    size = lax.axis_size("ctx")
    piece_index = jnp.arange(size, dtype=jnp.int32)
    return ((lax.axis_index("ctx") - (piece_index // 2) * 2) % size) ^ (piece_index % 2)


def ring_gather(own):
    laps = lax.axis_size("ctx") // 2
    if laps > longest_ring:
        placed = lax.all_gather(own, "ctx", axis=0)[piece_holders()]
        return [placed[i] for i in range(2 * laps)]
    pieces = []
    current = own
    for lap in range(laps):
        following = shift(current, "ctx", 2) if lap + 1 < laps else None
        pieces += [current, exchange(current, "ctx", 1)]
        current = following
    return pieces


def ring_reduce(chunks):
    laps = len(chunks) // 2
    if laps > longest_ring:
        every = jnp.arange(2 * laps, dtype=jnp.int32)
        piece_of = jnp.sum(
            jnp.where(piece_holders()[None, :] == every[:, None], every[None, :], 0), axis=1
        )
        placed = jnp.stack(chunks)[piece_of].astype(jnp.float32)
        return lax.psum_scatter(placed, "ctx", scatter_dimension=0)

    def pair_sum(lap):
        return chunks[2 * lap].astype(jnp.float32) + exchange(chunks[2 * lap + 1], "ctx", 1).astype(
            jnp.float32
        )

    moving = None
    for lap in list(range(1, laps)) + [0]:
        total = pair_sum(lap)
        if moving is not None:
            total = total + moving.astype(jnp.float32)
        if lap == 0:
            return total
        moving = shift(total.astype(jnp.bfloat16), "ctx", 2)


def local(
    tokens,
    pair_table,
    cotangent,
    heads_weight,
    merge_weight,
    gate_weight,
    up_weight,
    down_weight,
    norm_gains,
    heads_first,
    heads_second,
    merge_first,
    merge_second,
    gate_first,
    gate_second,
    up_first,
    up_second,
    down_first,
    down_second,
    gains_first,
    gains_second,
):
    bf16 = jnp.bfloat16
    f32 = jnp.float32
    context_size = lax.axis_size("ctx")
    shard_size = lax.axis_size("fsdp")
    shard_rank = lax.axis_index("fsdp")
    ranks = context_size * shard_size
    local_rows = tokens.shape[1]
    half_len = local_rows // 2
    seq_len = local_rows * context_size
    heads_own = heads_weight.shape[0]
    merge_own = merge_weight.shape[0]
    feed_own = gate_weight.shape[0]
    gains_own = norm_gains.shape[0]
    gain_rows = 8

    own_tokens = tokens[0]
    token_pieces = ring_gather(own_tokens)

    gain_block = jnp.pad(norm_gains[None, :], ((0, gain_rows - 1), (0, D - gains_own)))
    early = jnp.concatenate([heads_weight, gain_block], axis=0)
    early_pieces = ring_gather(jnp.concatenate([early, exchange(early, "fsdp", 2)], axis=0))
    early_rows = heads_own + gain_rows
    early_mine = jnp.concatenate(early_pieces, axis=0)
    early_all = jnp.concatenate([early_mine, exchange(early_mine, "fsdp", 1)], axis=0).reshape(
        ranks, early_rows, D
    )

    late = jnp.concatenate([merge_weight, gate_weight, up_weight, down_weight], axis=0)
    late_rows = merge_own + 3 * feed_own
    late_pieces = ring_gather(jnp.concatenate([late, exchange(late, "fsdp", 2)], axis=0))
    late_mine = jnp.stack(late_pieces, axis=0).reshape(2 * context_size, late_rows, D)
    merge_mine = late_mine[:, :merge_own]
    merge_blocks = jnp.concatenate([merge_mine, exchange(merge_mine, "fsdp", 1)], axis=0)

    piece_source = piece_holders()
    core_bit = jnp.arange(2, dtype=jnp.int32)
    rank_of_relative = (
        piece_source[None, :, None] * shard_size
        + (shard_rank ^ core_bit[:, None, None] ^ (2 * core_bit[None, None, :]))
    ).reshape(ranks)
    every_rank = jnp.arange(ranks, dtype=jnp.int32)
    relative_of_rank = jnp.sum(
        jnp.where(rank_of_relative[None, :] == every_rank[:, None], every_rank[None, :], 0), axis=1
    )

    pair_of_piece = pair_table[piece_source]
    blocks_of_piece = jnp.stack([pair_of_piece, 2 * context_size - 1 - pair_of_piece], axis=1)
    offsets = jnp.arange(half_len, dtype=jnp.int32)
    key_places = (blocks_of_piece[:, :, None] * half_len + offsets).reshape(seq_len)
    my_places = key_places[:local_rows]

    early_placed = early_all[relative_of_rank]
    heads_matrix = early_placed[:, :heads_own].reshape(ranks * heads_own, D)
    gain_vector = early_placed[:, heads_own, :gains_own].reshape(ranks * gains_own).astype(f32)
    query_matrix = heads_matrix[: HEADS * HD]
    pair_matrix = heads_matrix[HEADS * HD :]

    all_inputs = jnp.concatenate(token_pieces, axis=0)
    inputs = own_tokens.astype(f32)
    normed_all = normalize(all_inputs.astype(f32), gain_vector[0:D]).astype(bf16)
    normed_low = normed_all[:local_rows]
    pull_normed = jax.vjp(normalize, inputs, gain_vector[0:D])[1]
    projected_query = contract_cols(normed_low, query_matrix)
    projected_pair = contract_cols(normed_all, pair_matrix)

    def query_path(projected_rows, query_gain):
        rows = projected_rows.reshape(local_rows, HEADS, HD)
        return rotary(normalize(rows, query_gain), my_places).reshape(local_rows, HEADS * HD)

    def key_path(projected_rows, key_gain):
        return rotary(normalize(projected_rows, key_gain), key_places)

    queries, pull_query = jax.vjp(query_path, projected_query, gain_vector[4 * D : 4 * D + HD])
    keys, pull_key = jax.vjp(key_path, projected_pair[:, :HD], gain_vector[4 * D + HD :])

    def to_heads(per_row):
        return jnp.concatenate([per_row[:, h * HD : (h + 1) * HD] for h in range(HEADS)], axis=0)

    def to_rows(per_head):
        return jnp.concatenate(
            [per_head[h * local_rows : (h + 1) * local_rows] for h in range(HEADS)], axis=1
        )

    query_low = to_heads(queries.astype(bf16))
    key_low = keys.astype(bf16)
    value_low = projected_pair[:, HD:].astype(bf16)

    head_places = jnp.concatenate([my_places] * HEADS)
    allowed = key_places[None, :] <= head_places[:, None]
    scores = jnp.where(allowed, contract_cols(query_low, key_low) * score_scale, masked_score)
    row_max = jnp.max(scores, axis=-1, keepdims=True)
    log_total = row_max + jnp.log(jnp.sum(jnp.exp(scores - row_max), axis=-1, keepdims=True))
    weights = jnp.exp(scores - log_total)
    weights_low = weights.astype(bf16)
    attended = matmul(weights_low, value_low)
    attended_low = to_rows(attended.astype(bf16))
    merge_matrix = merge_blocks[relative_of_rank].reshape(ranks * merge_own, D)
    branch = matmul(attended_low, merge_matrix)

    def middle(inputs_rows, branch_rows, post_gain, ffn_gain):
        residual = inputs_rows + normalize(branch_rows, post_gain)
        return (residual, normalize(residual, ffn_gain))

    (residual, normed_ffn), pull_middle = jax.vjp(
        middle, inputs, branch, gain_vector[D : 2 * D], gain_vector[2 * D : 3 * D]
    )
    own_ffn_low = normed_ffn.astype(bf16)

    def both_cores(own_rows):
        return jnp.concatenate([own_rows, exchange(own_rows, "fsdp", 1)], axis=0)

    def core_sum(partial_rows):
        return partial_rows[:local_rows] + exchange(partial_rows[local_rows:], "fsdp", 1)

    hidden_mine = 2 * context_size * feed_own
    gate_matrix = late_mine[:, merge_own : merge_own + feed_own].reshape(hidden_mine, D)
    up_matrix = late_mine[:, merge_own + feed_own : merge_own + 2 * feed_own].reshape(
        hidden_mine, D
    )
    down_matrix = late_mine[:, merge_own + 2 * feed_own :].reshape(hidden_mine, D)
    ffn_low = both_cores(own_ffn_low)
    gate_values = contract_cols(ffn_low, gate_matrix)
    upward = contract_cols(ffn_low, up_matrix)

    def activate(gate_rows, upward_rows):
        return jax.nn.gelu(gate_rows, approximate=True) * upward_rows

    hidden, pull_activate = jax.vjp(activate, gate_values, upward)
    hidden_low = hidden.astype(bf16)
    output = core_sum(matmul(hidden_low, down_matrix))

    def finish(residual_rows, output_rows, out_gain):
        return residual_rows + normalize(output_rows, out_gain)

    block_out, pull_finish = jax.vjp(finish, residual, output, gain_vector[3 * D : 4 * D])
    upstream = cotangent[0].astype(f32)
    residual_slope, output_slope, final_gain_slope = pull_finish(upstream)
    output_low = both_cores(output_slope.astype(bf16))
    hidden_slope = contract_cols(output_low, down_matrix)
    gate_slope, upward_slope = pull_activate(hidden_slope)
    gate_low = gate_slope.astype(bf16)
    upward_low = upward_slope.astype(bf16)
    normed_ffn_slope = core_sum(matmul(gate_low, gate_matrix) + matmul(upward_low, up_matrix))
    feed_terms = jnp.concatenate(
        [
            contract_rows(left, right).astype(bf16).reshape(2 * context_size, feed_own, D)
            for left, right in (
                (gate_low, ffn_low),
                (upward_low, ffn_low),
                (hidden_low, output_low),
            )
        ],
        axis=1,
    ).reshape(context_size, 6 * feed_own, D)
    feed_pair = ring_reduce([feed_terms[i] for i in range(context_size)])

    def other_y(pair_rows):
        rows = pair_rows.shape[0] // 2
        return pair_rows[:rows] + exchange(pair_rows[rows:].astype(bf16), "fsdp", 2).astype(f32)

    feed_shard = other_y(feed_pair)

    input_slope, branch_slope, post_gain_slope, ffn_gain_slope = pull_middle(
        (residual_slope, normed_ffn_slope)
    )
    branch_low = branch_slope.astype(bf16)
    merge_terms = contract_rows(attended_low, branch_low)
    slope_low = to_heads(contract_cols(branch_low, merge_matrix).astype(bf16))
    row_delta = jnp.sum(slope_low.astype(f32) * attended, axis=-1, keepdims=True)
    weight_slope = contract_cols(slope_low, value_low)
    score_slope = (weights * (weight_slope - row_delta)).astype(bf16)
    query_slope = matmul(score_slope, key_low) * score_scale
    key_slope = contract_rows(score_slope, query_low) * score_scale
    value_slope = contract_rows(weights_low, slope_low)
    projected_query_slope, query_gain_slope = pull_query(to_rows(query_slope))
    projected_key_slope, key_gain_slope = pull_key(key_slope)
    query_slope_low = projected_query_slope.astype(bf16)
    pair_slope_low = jnp.concatenate(
        [projected_key_slope.astype(bf16), value_slope.astype(bf16)], axis=1
    )
    heads_terms = jnp.concatenate(
        [contract_rows(query_slope_low, normed_low), contract_rows(pair_slope_low, normed_all)],
        axis=0,
    )
    pre_gain_slope = (
        jnp.sum(heads_terms * heads_matrix.astype(f32), axis=0) / gain_vector[0:D]
    )
    gain_terms = jnp.concatenate(
        [
            pre_gain_slope,
            post_gain_slope,
            ffn_gain_slope,
            final_gain_slope,
            query_gain_slope,
            key_gain_slope,
        ]
    ).reshape(ranks, 1, gains_own)
    gain_padded = jnp.pad(
        gain_terms.astype(bf16), ((0, 0), (0, gain_rows - 1), (0, D - gains_own))
    )
    rest_own = heads_own + merge_own + gain_rows
    rest_terms = jnp.concatenate(
        [
            heads_terms.astype(bf16).reshape(ranks, heads_own, D),
            merge_terms.astype(bf16).reshape(ranks, merge_own, D),
            gain_padded,
        ],
        axis=1,
    )[rank_of_relative].reshape(2, context_size, 2 * rest_own, D)
    rest_sum = (
        rest_terms[0].astype(f32) + exchange(rest_terms[1], "fsdp", 1).astype(f32)
    ).astype(bf16)
    rest_shard = other_y(ring_reduce([rest_sum[i] for i in range(context_size)]))

    pair_own = ring_reduce(
        [pair_slope_low[i * local_rows : (i + 1) * local_rows] for i in range(context_size)]
    ).astype(bf16)
    normed_slope = matmul(query_slope_low, query_matrix) + matmul(pair_own, pair_matrix)
    tokens_gradient = (input_slope + pull_normed(normed_slope)[0])[None]

    heads_shard = rest_shard[:heads_own]
    merge_shard = rest_shard[heads_own : heads_own + merge_own]
    gains_shard = rest_shard[heads_own + merge_own, :gains_own]
    gate_shard = feed_shard[:feed_own]
    up_shard = feed_shard[feed_own : 2 * feed_own]
    down_shard = feed_shard[2 * feed_own :]
    heads_out = adamw(heads_weight, heads_shard, heads_first, heads_second)
    merge_out = adamw(merge_weight, merge_shard, merge_first, merge_second)
    gate_out = adamw(gate_weight, gate_shard, gate_first, gate_second)
    up_out = adamw(up_weight, up_shard, up_first, up_second)
    down_out = adamw(down_weight, down_shard, down_first, down_second)
    gains_out = adamw(norm_gains, gains_shard, gains_first, gains_second)
    mixed = block_out.astype(jnp.bfloat16)[None]
    return (
        mixed,
        tokens_gradient,
        heads_out[0],
        heads_out[1],
        heads_out[2],
        heads_out[3],
        merge_out[0],
        merge_out[1],
        merge_out[2],
        merge_out[3],
        gate_out[0],
        gate_out[1],
        gate_out[2],
        gate_out[3],
        up_out[0],
        up_out[1],
        up_out[2],
        up_out[3],
        down_out[0],
        down_out[1],
        down_out[2],
        down_out[3],
        gains_out[0],
        gains_out[1],
        gains_out[2],
        gains_out[3],
    )


def solution(mesh):
    in_specs = (
        P("fsdp", "ctx", None),
        P(),
        P("fsdp", "ctx", None),
        P(("ctx", "fsdp"), None),
        P(("ctx", "fsdp"), None),
        P(("ctx", "fsdp"), None),
        P(("ctx", "fsdp"), None),
        P(("ctx", "fsdp"), None),
        P(("ctx", "fsdp")),
        P(("ctx", "fsdp"), None),
        P(("ctx", "fsdp"), None),
        P(("ctx", "fsdp"), None),
        P(("ctx", "fsdp"), None),
        P(("ctx", "fsdp"), None),
        P(("ctx", "fsdp"), None),
        P(("ctx", "fsdp"), None),
        P(("ctx", "fsdp"), None),
        P(("ctx", "fsdp"), None),
        P(("ctx", "fsdp"), None),
        P(("ctx", "fsdp")),
        P(("ctx", "fsdp")),
    )
    out_specs = (
        P("fsdp", "ctx", None),
        P("fsdp", "ctx", None),
        P(("ctx", "fsdp"), None),
        P(("ctx", "fsdp"), None),
        P(("ctx", "fsdp"), None),
        P(("ctx", "fsdp"), None),
        P(("ctx", "fsdp"), None),
        P(("ctx", "fsdp"), None),
        P(("ctx", "fsdp"), None),
        P(("ctx", "fsdp"), None),
        P(("ctx", "fsdp"), None),
        P(("ctx", "fsdp"), None),
        P(("ctx", "fsdp"), None),
        P(("ctx", "fsdp"), None),
        P(("ctx", "fsdp"), None),
        P(("ctx", "fsdp"), None),
        P(("ctx", "fsdp"), None),
        P(("ctx", "fsdp"), None),
        P(("ctx", "fsdp"), None),
        P(("ctx", "fsdp"), None),
        P(("ctx", "fsdp"), None),
        P(("ctx", "fsdp"), None),
        P(("ctx", "fsdp")),
        P(("ctx", "fsdp")),
        P(("ctx", "fsdp")),
        P(("ctx", "fsdp")),
    )
    return jax.shard_map(local, mesh=mesh, in_specs=in_specs, out_specs=out_specs, check_vma=False)
```

```python
import jax
import jax.numpy as jnp
from jax import lax
from jax.sharding import PartitionSpec as P

D = 640
HEADS = 4
HD = 256
STEP = 3


norm_eps = 1e-06
rope_base = 1000000.0
score_scale = 0.0625
masked_score = -1e30
beta_one = 0.9
beta_two = 0.95
learn_rate = 0.02
weight_decay = 0.1
adam_eps = 1e-08


def normalize(values, norm_gain):
    return (
        values * lax.rsqrt(jnp.mean(values * values, axis=-1, keepdims=True) + norm_eps) * norm_gain
    )


def rotary(values, positions):
    extent = values.shape[-1]
    half_width = extent // 2
    frequency = rope_base ** (-(jnp.arange(half_width, dtype=jnp.float32) * 2.0 / extent))
    angles = positions.astype(jnp.float32)[:, None] * frequency[None, :]
    target_shape = (values.shape[0],) + (1,) * (values.ndim - 2) + (extent,)
    cosine_part = jnp.concatenate([jnp.cos(angles), jnp.cos(angles)], axis=-1).reshape(target_shape)
    sine_part = jnp.concatenate([jnp.sin(angles), jnp.sin(angles)], axis=-1).reshape(target_shape)
    turned = jnp.concatenate([-values[..., half_width:], values[..., :half_width]], axis=-1)
    return values * cosine_part + turned * sine_part


def matmul(former, latter):
    return jnp.dot(former, latter, preferred_element_type=jnp.float32)


def contract_rows(former, latter):
    return lax.dot_general(
        former, latter, (((0,), (0,)), ((), ())), preferred_element_type=jnp.float32
    )


def contract_cols(former, latter):
    return lax.dot_general(
        former, latter, (((1,), (1,)), ((), ())), preferred_element_type=jnp.float32
    )


def adamw(weight, gradient, momentum, variance):
    moment_new = beta_one * momentum + (1.0 - beta_one) * gradient
    variance_new = beta_two * variance + (1.0 - beta_two) * gradient * gradient
    corrected = moment_new / (1.0 - beta_one**STEP)
    spread = jnp.sqrt(variance_new / (1.0 - beta_two**STEP))
    update = -learn_rate * (
        corrected / (spread + adam_eps) + weight_decay * weight.astype(jnp.float32)
    )
    return (gradient, update, moment_new, variance_new)


longest_ring = 4


def exchange(values, axis, step):
    return lax.ppermute(values, axis, [(i, i ^ step) for i in range(lax.axis_size(axis))])


def shift(values, axis, step):
    size = lax.axis_size(axis)
    return lax.ppermute(values, axis, [(i, (i + step) % size) for i in range(size)])


def after(values, *others):
    return lax.optimization_barrier((values, *others))[0]


def holder(lap, side):
    size = lax.axis_size("ctx")
    return ((lax.axis_index("ctx") - 2 * lap) % size) ^ side


def by_bit(bit, first, second):
    return jnp.where(bit == 0, jnp.stack([first, second]), jnp.stack([second, first]))


def ring_gather(own, gates):
    laps = lax.axis_size("ctx") // 2
    if laps > longest_ring:
        return [(0, lax.all_gather(own, "ctx", axis=0))]
    pieces = []
    current = own
    for lap in range(laps):
        current = after(current, *gates.get(lap, ()))
        following = shift(current, "ctx", 2) if lap + 1 < laps else None
        crossed = exchange(current, "ctx", 1)
        pieces += [(holder(lap, 0), current[None]), (holder(lap, 1), crossed[None])]
        current = following
    return pieces


def place(buffer, index, pieces):
    start = (index,) + (0,) * (buffer.ndim - 1)
    return lax.dynamic_update_slice(buffer, pieces.astype(buffer.dtype), start)


def ring_reduce(terms, gates):
    laps = terms.shape[0] // 2
    if laps > longest_ring:
        return lax.psum_scatter(terms.astype(jnp.float32), "ctx", scatter_dimension=0)

    def chunk(lap, side):
        return lax.dynamic_index_in_dim(terms, holder(lap, side), 0, keepdims=False)

    moving = None
    crossed = None
    for lap in list(range(1, laps)) + [0]:
        sent = chunk(lap, 1).astype(jnp.bfloat16)
        held = gates.get(lap, ())
        if crossed is not None:
            held = (crossed, *held)
        sent = after(sent, *held) if held else sent
        crossed = exchange(sent, "ctx", 1)
        total = chunk(lap, 0).astype(jnp.float32) + crossed.astype(jnp.float32)
        if moving is not None:
            total = total + moving.astype(jnp.float32)
        if lap == 0:
            return total
        moving = shift(total.astype(jnp.bfloat16), "ctx", 2)


def local(
    tokens,
    pair_table,
    cotangent,
    heads_weight,
    merge_weight,
    gate_weight,
    up_weight,
    down_weight,
    norm_gains,
    heads_first,
    heads_second,
    merge_first,
    merge_second,
    gate_first,
    gate_second,
    up_first,
    up_second,
    down_first,
    down_second,
    gains_first,
    gains_second,
):
    bf16 = jnp.bfloat16
    f32 = jnp.float32
    context_size = lax.axis_size("ctx")
    shard_size = lax.axis_size("fsdp")
    shard_rank = lax.axis_index("fsdp")
    core_bit = shard_rank % 2
    y_bit = shard_rank // 2
    ranks = context_size * shard_size
    local_rows = tokens.shape[1]
    half_len = local_rows // 2
    seq_len = local_rows * context_size
    heads_own = heads_weight.shape[0]
    merge_own = merge_weight.shape[0]
    feed_own = gate_weight.shape[0]
    gains_own = norm_gains.shape[0]
    gain_rows = 8

    def place_of(pair):
        blocks = jnp.stack([pair, 2 * context_size - 1 - pair], axis=-1)
        offsets = jnp.arange(half_len, dtype=jnp.int32)
        return (blocks[..., None] * half_len + offsets).reshape(-1)

    key_places = place_of(pair_table)
    my_places = place_of(pair_table[lax.axis_index("ctx")])

    own_tokens = tokens[0]
    gain_block = jnp.pad(norm_gains[None, :], ((0, gain_rows - 1), (0, D - gains_own)))
    early = jnp.concatenate([heads_weight, merge_weight, gain_block], axis=0)
    early_rows = early.shape[0]
    early_pair = by_bit(y_bit, early, exchange(early, "fsdp", 2))
    early_pieces = ring_gather(
        jnp.concatenate([early_pair.reshape(2 * early_rows, D), own_tokens], axis=0), {}
    )
    heads_buffer = jnp.zeros((context_size, shard_size, heads_own, D), bf16)
    merge_buffer = jnp.zeros((context_size, shard_size, merge_own, D), bf16)
    gain_buffer = jnp.zeros((context_size, shard_size, 1, D), bf16)
    token_buffer = jnp.zeros((context_size, local_rows, D), bf16)
    for index, pieces in early_pieces:
        mine = pieces[:, : 2 * early_rows]
        both = by_bit(core_bit, mine, exchange(mine, "fsdp", 1))
        both = both.reshape(2, -1, 2, early_rows, D).transpose(1, 2, 0, 3, 4)
        both = both.reshape(-1, shard_size, early_rows, D)
        heads_buffer = place(heads_buffer, index, both[:, :, :heads_own])
        merge_buffer = place(merge_buffer, index, both[:, :, heads_own : heads_own + merge_own])
        gain_buffer = place(gain_buffer, index, both[:, :, heads_own + merge_own :][:, :, :1])
        token_buffer = place(token_buffer, index, pieces[:, 2 * early_rows :])
    heads_matrix = heads_buffer.reshape(ranks * heads_own, D)
    merge_matrix = merge_buffer.reshape(ranks * merge_own, D)
    gain_vector = gain_buffer[:, :, 0, :gains_own].reshape(ranks * gains_own).astype(f32)
    all_inputs = token_buffer.reshape(seq_len, D)
    query_matrix = heads_matrix[: HEADS * HD]
    pair_matrix = heads_matrix[HEADS * HD :]

    inputs = own_tokens.astype(f32)
    normed_all = normalize(all_inputs.astype(f32), gain_vector[0:D]).astype(bf16)
    normed, pull_normed = jax.vjp(normalize, inputs, gain_vector[0:D])
    normed_low = normed.astype(bf16)
    projected_query = contract_cols(normed_low, query_matrix)
    projected_pair = contract_cols(normed_all, pair_matrix)

    def to_heads(per_row):
        return jnp.concatenate([per_row[:, h * HD : (h + 1) * HD] for h in range(HEADS)], axis=0)

    def to_rows(per_head):
        return jnp.concatenate(
            [per_head[h * local_rows : (h + 1) * local_rows] for h in range(HEADS)], axis=1
        )

    head_places = jnp.concatenate([my_places] * HEADS)

    def query_path(projected_rows, query_gain):
        return rotary(normalize(projected_rows, query_gain), head_places)

    def key_path(projected_rows, key_gain):
        return rotary(normalize(projected_rows, key_gain), key_places)

    queries, pull_query = jax.vjp(
        query_path, to_heads(projected_query), gain_vector[4 * D : 4 * D + HD]
    )
    keys, pull_key = jax.vjp(key_path, projected_pair[:, :HD], gain_vector[4 * D + HD :])
    query_low = queries.astype(bf16)
    key_low = keys.astype(bf16)
    value_low = projected_pair[:, HD:].astype(bf16)

    allowed = key_places[None, :] <= head_places[:, None]
    scores = jnp.where(allowed, contract_cols(query_low, key_low) * score_scale, masked_score)
    row_max = jnp.max(scores, axis=-1, keepdims=True)
    log_total = row_max + jnp.log(jnp.sum(jnp.exp(scores - row_max), axis=-1, keepdims=True))
    weights = jnp.exp(scores - log_total)
    weights_low = weights.astype(bf16)
    attended = matmul(weights_low, value_low)
    attended_low = to_rows(attended.astype(bf16))
    branch = matmul(attended_low, merge_matrix)

    late = jnp.stack([gate_weight, up_weight, down_weight])
    with jax.named_scope("late"):
        late_pieces = ring_gather(late, {0: (early_pieces[-2:][0][1],), 2: (projected_pair,)})
    stacked = jnp.concatenate([pieces for _, pieces in late_pieces], axis=0)
    hidden_mine = context_size * feed_own
    gate_up = stacked[:, :2].transpose(1, 0, 2, 3).reshape(2 * hidden_mine, D)
    down_matrix = stacked[:, 2].reshape(hidden_mine, D)

    def middle(inputs_rows, branch_rows, post_gain, ffn_gain):
        residual = inputs_rows + normalize(branch_rows, post_gain)
        return (residual, normalize(residual, ffn_gain))

    (residual, normed_ffn), pull_middle = jax.vjp(
        middle, inputs, branch, gain_vector[D : 2 * D], gain_vector[2 * D : 3 * D]
    )

    def all_sequences(own_rows):
        pair_rows = jnp.concatenate([own_rows, exchange(own_rows, "fsdp", 2)], axis=0)
        return jnp.concatenate([pair_rows, exchange(pair_rows, "fsdp", 1)], axis=0)

    def sequence_sum(partial_rows):
        pair_rows = partial_rows[: 2 * local_rows] + exchange(
            partial_rows[2 * local_rows :], "fsdp", 1
        )
        sent = pair_rows[local_rows:].astype(bf16)
        return pair_rows[:local_rows] + exchange(sent, "fsdp", 2).astype(f32)

    ffn_low = all_sequences(normed_ffn.astype(bf16))
    gate_up_values = contract_cols(ffn_low, gate_up)

    def activate(both_values):
        gate_rows = both_values[:, :hidden_mine]
        return jax.nn.gelu(gate_rows, approximate=True) * both_values[:, hidden_mine:]

    hidden, pull_activate = jax.vjp(activate, gate_up_values)
    hidden_low = hidden.astype(bf16)
    output = sequence_sum(matmul(hidden_low, down_matrix))

    def finish(residual_rows, output_rows, out_gain):
        return residual_rows + normalize(output_rows, out_gain)

    block_out, pull_finish = jax.vjp(finish, residual, output, gain_vector[3 * D : 4 * D])
    upstream = cotangent[0].astype(f32)
    residual_slope, output_slope, final_gain_slope = pull_finish(upstream)
    output_low = all_sequences(output_slope.astype(bf16))
    hidden_slope = contract_cols(output_low, down_matrix)
    gate_up_low = pull_activate(hidden_slope)[0].astype(bf16)
    normed_ffn_slope = sequence_sum(matmul(gate_up_low, gate_up))
    gate_up_terms = contract_rows(gate_up_low, ffn_low).astype(bf16)
    down_terms = contract_rows(hidden_low, output_low).astype(bf16)

    input_slope, branch_slope, post_gain_slope, ffn_gain_slope = pull_middle(
        (residual_slope, normed_ffn_slope)
    )
    branch_low = branch_slope.astype(bf16)
    merge_terms = contract_rows(attended_low, branch_low)
    slope_low = to_heads(contract_cols(branch_low, merge_matrix).astype(bf16))
    row_delta = jnp.sum(slope_low.astype(f32) * attended, axis=-1, keepdims=True)
    weight_slope = contract_cols(slope_low, value_low)
    score_slope = (weights * (weight_slope - row_delta)).astype(bf16)
    query_slope = matmul(score_slope, key_low) * score_scale
    key_slope = contract_rows(score_slope, query_low) * score_scale
    value_slope = contract_rows(weights_low, slope_low)
    projected_query_slope, query_gain_slope = pull_query(query_slope)
    projected_key_slope, key_gain_slope = pull_key(key_slope)
    query_slope_low = to_rows(projected_query_slope.astype(bf16))
    pair_slope_low = jnp.concatenate(
        [projected_key_slope.astype(bf16), value_slope.astype(bf16)], axis=1
    )
    heads_terms = jnp.concatenate(
        [contract_rows(query_slope_low, normed_low), contract_rows(pair_slope_low, normed_all)],
        axis=0,
    )
    pre_gain_slope = jnp.sum(heads_terms * heads_matrix.astype(f32), axis=0) / gain_vector[0:D]

    def feed_reduce():
        gate_up_parts = gate_up_terms.reshape(2, context_size, feed_own, D)
        down_parts = down_terms.reshape(1, context_size, feed_own, D)
        laps = context_size // 2
        if laps > longest_ring:
            parts = jnp.concatenate([gate_up_parts, down_parts]).transpose(1, 0, 2, 3)
            return lax.psum_scatter(parts.astype(f32), "ctx", scatter_dimension=0)

        def chunk(lap, side):
            piece = 2 * lap + side
            return jnp.concatenate([gate_up_parts[:, piece], down_parts[:, piece]])

        gates = {2: (branch_low,), 3: (score_slope,), 0: (key_slope,)}
        moving = None
        crossed = None
        for lap in list(range(1, laps)) + [0]:
            sent = chunk(lap, 1)
            if crossed is not None:
                sent = after(sent, crossed, *gates.get(lap, ()))
            crossed = exchange(sent, "ctx", 1)
            total = chunk(lap, 0).astype(f32) + crossed.astype(f32)
            if moving is not None:
                total = total + moving.astype(f32)
            if lap == 0:
                return total
            moving = shift(total.astype(bf16), "ctx", 2)

    def y_sum(pair_rows):
        kept = jnp.where(y_bit == 0, pair_rows[0], pair_rows[1])
        sent = jnp.where(y_bit == 0, pair_rows[1], pair_rows[0]).astype(bf16)
        return kept + exchange(sent, "fsdp", 2).astype(f32)

    feed_shard = feed_reduce()

    pair_own = ring_reduce(
        pair_slope_low.reshape(context_size, local_rows, 2 * HD), {}
    ).astype(bf16)

    gain_terms = jnp.concatenate(
        [
            pre_gain_slope,
            post_gain_slope,
            ffn_gain_slope,
            final_gain_slope,
            query_gain_slope,
            key_gain_slope,
        ]
    ).reshape(ranks, 1, gains_own)
    gain_padded = jnp.pad(gain_terms, ((0, 0), (0, gain_rows - 1), (0, D - gains_own)))

    def by_core(terms, rows):
        parts = terms.reshape(context_size, 2, 2, rows, D)
        kept = jnp.where(core_bit == 0, parts[:, :, 0], parts[:, :, 1])
        sent = jnp.where(core_bit == 0, parts[:, :, 1], parts[:, :, 0]).astype(bf16)
        return kept, sent

    rest_parts = [
        by_core(heads_terms, heads_own),
        by_core(merge_terms, merge_own),
        by_core(gain_padded, gain_rows),
    ]
    rest_crossed = exchange(
        jnp.concatenate([part[1] for part in rest_parts], axis=2), "fsdp", 1
    )
    rest_sum = (
        jnp.concatenate([part[0] for part in rest_parts], axis=2) + rest_crossed.astype(f32)
    ).astype(bf16)
    rest_shard = y_sum(ring_reduce(rest_sum, {}))

    normed_slope = matmul(query_slope_low, query_matrix) + matmul(pair_own, pair_matrix)
    tokens_gradient = (input_slope + pull_normed(normed_slope)[0])[None]

    heads_shard = rest_shard[:heads_own]
    merge_shard = rest_shard[heads_own : heads_own + merge_own]
    gains_shard = rest_shard[heads_own + merge_own, :gains_own]
    gate_shard = feed_shard[0]
    up_shard = feed_shard[1]
    down_shard = feed_shard[2]
    heads_out = adamw(heads_weight, heads_shard, heads_first, heads_second)
    merge_out = adamw(merge_weight, merge_shard, merge_first, merge_second)
    gate_out = adamw(gate_weight, gate_shard, gate_first, gate_second)
    up_out = adamw(up_weight, up_shard, up_first, up_second)
    down_out = adamw(down_weight, down_shard, down_first, down_second)
    gains_out = adamw(norm_gains, gains_shard, gains_first, gains_second)
    mixed = block_out.astype(jnp.bfloat16)[None]
    return (
        mixed,
        tokens_gradient,
        heads_out[0],
        heads_out[1],
        heads_out[2],
        heads_out[3],
        merge_out[0],
        merge_out[1],
        merge_out[2],
        merge_out[3],
        gate_out[0],
        gate_out[1],
        gate_out[2],
        gate_out[3],
        up_out[0],
        up_out[1],
        up_out[2],
        up_out[3],
        down_out[0],
        down_out[1],
        down_out[2],
        down_out[3],
        gains_out[0],
        gains_out[1],
        gains_out[2],
        gains_out[3],
    )


def solution(mesh):
    in_specs = (
        P("fsdp", "ctx", None),
        P(),
        P("fsdp", "ctx", None),
        P(("ctx", "fsdp"), None),
        P(("ctx", "fsdp"), None),
        P(("ctx", "fsdp"), None),
        P(("ctx", "fsdp"), None),
        P(("ctx", "fsdp"), None),
        P(("ctx", "fsdp")),
        P(("ctx", "fsdp"), None),
        P(("ctx", "fsdp"), None),
        P(("ctx", "fsdp"), None),
        P(("ctx", "fsdp"), None),
        P(("ctx", "fsdp"), None),
        P(("ctx", "fsdp"), None),
        P(("ctx", "fsdp"), None),
        P(("ctx", "fsdp"), None),
        P(("ctx", "fsdp"), None),
        P(("ctx", "fsdp"), None),
        P(("ctx", "fsdp")),
        P(("ctx", "fsdp")),
    )
    out_specs = (
        P("fsdp", "ctx", None),
        P("fsdp", "ctx", None),
        P(("ctx", "fsdp"), None),
        P(("ctx", "fsdp"), None),
        P(("ctx", "fsdp"), None),
        P(("ctx", "fsdp"), None),
        P(("ctx", "fsdp"), None),
        P(("ctx", "fsdp"), None),
        P(("ctx", "fsdp"), None),
        P(("ctx", "fsdp"), None),
        P(("ctx", "fsdp"), None),
        P(("ctx", "fsdp"), None),
        P(("ctx", "fsdp"), None),
        P(("ctx", "fsdp"), None),
        P(("ctx", "fsdp"), None),
        P(("ctx", "fsdp"), None),
        P(("ctx", "fsdp"), None),
        P(("ctx", "fsdp"), None),
        P(("ctx", "fsdp"), None),
        P(("ctx", "fsdp"), None),
        P(("ctx", "fsdp"), None),
        P(("ctx", "fsdp"), None),
        P(("ctx", "fsdp")),
        P(("ctx", "fsdp")),
        P(("ctx", "fsdp")),
        P(("ctx", "fsdp")),
    )
    return jax.shard_map(local, mesh=mesh, in_specs=in_specs, out_specs=out_specs, check_vma=False)
```
